32 devices in a mesh: seq: 8 (over y, x, core), dp: 4 (over z).
Axes of the slice: x: 2, y: 2, z: 4, core: 2. Of those that a mesh axis runs over, the one named last changes fastest.
Arguments:
- inputs: bfloat16 [4, 4096, 1024], P('dp', 'seq'), may hold values from -600 to 600
- cotangent: bfloat16 [4, 4096, 1024], P('dp', 'seq'), may hold values from -6 to 6
- gain: float32 [1024], replicated, may hold values from 0.5 to 1.5
- w_qkv: bfloat16 [1024, 3072], replicated, may hold values from -1.25 to 1.25
- w_out: bfloat16 [1024, 1024], replicated, may hold values from -0.1875 to 0.1875
- segment_ids: int32 [4, 4096], P('dp'), may hold values from 0 to 3, never falling along the last dimension, each value on 1 to 2048 neighbouring positions
Outputs:
- grad_inputs: bfloat16 [4, 4096, 1024], P('dp', 'seq')
- grad_qkv_weight: float32 [1024, 3072], P('seq')
The draws below stay inside these ranges and needn't reach their ends.
Inputs may be any that keep to these rules, and one draw needn't show every extreme that they name: `segment_ids`: each row is non-decreasing; every document is 1 to 2048 bytes long and one is exactly 2048.
All inputs are finite; a program needn't handle non-finite values.
Results may differ from the reference program's by a relative error of at most 0.03.
Values may be sent and summed in bfloat16 or wider, within the bound.
No kernel may reach another device: no remote copies, remote signals or barrier semaphores. Data moves between devices by JAX's collectives and lax.ppermute only.
A program may use at most 192 MiB of HBM per device.

```python
import math
import jax
import jax.numpy as jnp
import numpy as np
from jax import lax

D = 1024
HEADS = 16
WINDOW = 512
TOK_DEV = 512
SEQLEN = 4096
DOCS = 4
DOC_MOST = 2048
N_DP = 4


def draw_inputs(key, part):
    first, second, third = jax.random.split(jax.random.fold_in(key, 11), 3)
    base = jnp.clip(jax.random.normal(first, (N_DP, SEQLEN, D), jnp.float32), -4.0, 4.0)
    row_scale = jnp.exp(jax.random.uniform(second, (N_DP, SEQLEN, 1), jnp.float32, 0.0, math.log(10.0)))
    col_scale = jnp.exp(jax.random.uniform(third, (D,), jnp.float32, 0.0, math.log(10.0)))
    return (base * row_scale * col_scale).astype(jnp.bfloat16)


def draw_w_qkv(key, part):
    first = jax.random.fold_in(jax.random.fold_in(key, 23), 0)
    base = jnp.clip(jax.random.normal(first, (D, 3 * D), jnp.float32), -5.0, 5.0) * D ** (-0.5)
    return base.astype(jnp.bfloat16)


def steps_of(rng, extent, cuts, least, top_value):
    def one(axis_at, blocks):
        draws = jax.random.uniform(jax.random.fold_in(jax.random.fold_in(rng, 6), axis_at), (blocks,), jnp.float32, least / len(cuts), top_value / len(cuts))
        return jnp.repeat(jnp.exp(draws), extent[axis_at] // blocks).reshape((-1,) + (1,) * (len(extent) - axis_at - 1))

    level = one(*cuts[0])
    for cut in cuts[1:]:
        level = level * one(*cut)
    return level


def length_profile(count, total, reach, lean):
    portions = [(1 << 20) // math.isqrt(standing ** lean) + 1 for standing in range(2, count + 1)]
    rest, holding = total - reach - (count - 1), [1] * (count - 1)
    while rest > 0:
        free = [i for i in range(count - 1) if holding[i] < reach]
        pool, left = sum([portions[i] for i in free]), rest
        for i in free:
            extra = min(reach - holding[i], max(1, left * portions[i] // pool), rest)
            holding[i] = holding[i] + extra
            rest = rest - extra
    return np.array([reach] + holding)


def uneven_parts(key, amount, total, bound, slope):
    if amount == 2:
        one = jax.random.randint(key, (), max(1, total - bound), min(bound, total - 1) + 1)
        return jnp.stack([one, total - one])
    tallies = jnp.asarray(length_profile(amount, total, bound, slope), jnp.int32)
    couples = (amount - 1) // 2
    source_of, sink = tallies[1:1 + 2 * couples:2], tallies[2:2 + 2 * couples:2]
    room = jnp.minimum(source_of - 1, bound - sink)
    moved = jax.random.randint(jax.random.fold_in(key, 1), (couples,), 0, 1 << 20) % (room + 1)
    tallies = tallies.at[1:1 + 2 * couples:2].set(source_of - moved).at[2:2 + 2 * couples:2].set(sink + moved)
    return tallies[jax.random.permutation(jax.random.fold_in(key, 2), amount)]


def noise(rng, extent, spread, most, cuts=(), held_as=jnp.bfloat16):
    factor_of = steps_of(rng, extent, cuts, -0.22, 0.18) if cuts else 1.0
    entries = jax.random.normal(rng, extent, jnp.float32) * spread * factor_of
    return jnp.minimum(jnp.maximum(entries, -most), most).astype(held_as)


def setup_inputs(seed: int = 0) -> dict:
    seeds = jax.random.split(jax.random.key(seed), 7)
    inputs = draw_inputs(jax.random.fold_in(seeds[6], 71), 0)
    cotangent = noise(seeds[1], (N_DP, SEQLEN, D), 1.0, 6.0, ((0, 4), (1, 8)))
    gain = jnp.clip(1.0 + 0.1 * jax.random.normal(seeds[2], (D,), jnp.float32), 0.5, 1.5)
    w_qkv = draw_w_qkv(jax.random.fold_in(seeds[6], 71), 0)
    w_out = noise(seeds[4], (D, D), D ** -0.5, 0.1875)
    segment_ids = jax.vmap(lambda own: jnp.searchsorted(jnp.cumsum(uneven_parts(own, DOCS, SEQLEN, DOC_MOST, 2)), jnp.arange(SEQLEN), side="right"))(jax.random.split(seeds[5], N_DP)).reshape((N_DP, SEQLEN)).astype(jnp.int32)
    return {"inputs": inputs, "cotangent": cotangent, "gain": gain, "w_qkv": w_qkv, "w_out": w_out, "segment_ids": segment_ids}


EPS = 1e-05

def soft_probs(qblk, kblk, pos_q, pos_k, seg_q, seg_k):
    qh = qblk.reshape(qblk.shape[0], HEADS, -1).astype(jnp.float32)
    kh = kblk.reshape(kblk.shape[0], HEADS, -1).astype(jnp.float32)
    scores = jnp.einsum('qhd,khd->hqk', qh, kh) * qh.shape[2] ** (-0.5)
    allowed = (pos_k[None, :] <= pos_q[:, None]) & (pos_q[:, None] - pos_k[None, :] < WINDOW) & (seg_k[None, :] == seg_q[:, None])
    scores = jnp.where(allowed[None], scores, -1e+30)
    top = lax.optimization_barrier(jnp.max(scores, axis=2, keepdims=True))
    expo = jnp.exp(scores - top)
    return expo / lax.optimization_barrier(jnp.sum(expo, axis=2, keepdims=True))

def lowered(value):
    return lax.optimization_barrier(value.astype(jnp.bfloat16)).astype(jnp.float32)

def one_sequence(x, grad_out, gain, w_qkv, w_out, seg):
    length = x.shape[0]
    width = x.shape[1]
    xf = x.astype(jnp.float32)
    inv_rms = lax.rsqrt(lax.optimization_barrier(jnp.mean(xf * xf, axis=1, keepdims=True)) + EPS)
    normal_x = xf * inv_rms
    normed = (normal_x * gain).astype(jnp.bfloat16)
    qkv = jnp.dot(normed, w_qkv, preferred_element_type=jnp.float32).astype(jnp.bfloat16)
    queries = qkv[:, :width]
    keys_pad = jnp.concatenate([jnp.zeros((WINDOW, width), jnp.bfloat16), qkv[:, width:2 * width]], 0)
    values_pad = jnp.concatenate([jnp.zeros((WINDOW, width), jnp.bfloat16), qkv[:, 2 * width:]], 0)
    seg_pad = jnp.concatenate([jnp.full((WINDOW,), -1, jnp.int32), seg.astype(jnp.int32)], 0)
    block = min(512, TOK_DEV)
    count = length // block
    span = WINDOW + block
    scale = (width // HEADS) ** (-0.5)

    def pieces(first):
        pos_q = (first + jnp.arange(block)).astype(jnp.int32)
        pos_k = (first - WINDOW + jnp.arange(span)).astype(jnp.int32)
        qblk = lax.dynamic_slice_in_dim(queries, first, block, 0)
        kblk = lax.dynamic_slice_in_dim(keys_pad, first, span, 0)
        vblk = lax.dynamic_slice_in_dim(values_pad, first, span, 0)
        seg_q = lax.dynamic_slice_in_dim(seg_pad, first + WINDOW, block, 0)
        seg_k = lax.dynamic_slice_in_dim(seg_pad, first, span, 0)
        probs = soft_probs(qblk, kblk, pos_q, pos_k, seg_q, seg_k)
        return (qblk, kblk, vblk, probs)

    def forward_block(index):
        first = (index * block).astype(jnp.int32)
        qblk, kblk, vblk, probs = pieces(first)
        vh = vblk.reshape(span, HEADS, -1).astype(jnp.float32)
        out = jnp.einsum('hqk,khd->qhd', lowered(probs), vh)
        return out.astype(jnp.bfloat16).reshape(block, width)
    attn = lax.map(forward_block, jnp.arange(count, dtype=jnp.int32)).reshape(length, width)
    d_attn = jnp.dot(grad_out, w_out.T, preferred_element_type=jnp.float32).astype(jnp.bfloat16)

    def accumulate(total, part, first):
        return lax.dynamic_update_slice_in_dim(total, lax.dynamic_slice_in_dim(total, first, span, 0) + part, first, 0)

    def backward_block(carry, index):
        own_k, own_v, cross_k, cross_v = carry
        first = (index * block).astype(jnp.int32)
        qblk, kblk, vblk, probs = pieces(first)
        qh = qblk.reshape(block, HEADS, -1).astype(jnp.float32)
        kh = kblk.reshape(span, HEADS, -1).astype(jnp.float32)
        vh = vblk.reshape(span, HEADS, -1).astype(jnp.float32)
        do_h = lax.dynamic_slice_in_dim(d_attn, first, block, 0).reshape(block, HEADS, -1).astype(jnp.float32)
        o_h = lax.dynamic_slice_in_dim(attn, first, block, 0).reshape(block, HEADS, -1).astype(jnp.float32)
        delta = lax.optimization_barrier(jnp.sum(do_h * o_h, axis=2))
        dprob = jnp.einsum('qhd,khd->hqk', do_h, vh)
        dscore = lowered(probs * (dprob - delta.T[:, :, None]) * scale)
        grad_q = jnp.einsum('hqk,khd->qhd', dscore, kh).astype(jnp.bfloat16).reshape(block, width)
        part_k = jnp.einsum('hqk,qhd->khd', dscore, qh).reshape(span, width)
        part_v = jnp.einsum('hqk,qhd->khd', lowered(probs), do_h).reshape(span, width)
        shard_start = first // TOK_DEV * TOK_DEV
        pos_k = (first - WINDOW + jnp.arange(span)).astype(jnp.int32)
        cross = (pos_k < shard_start)[:, None]
        zero = jnp.zeros((span, width), jnp.float32)
        own_k = accumulate(own_k, jnp.where(cross, zero, part_k), first)
        own_v = accumulate(own_v, jnp.where(cross, zero, part_v), first)
        cross_k = accumulate(cross_k, jnp.where(cross, part_k, zero), first)
        cross_v = accumulate(cross_v, jnp.where(cross, part_v, zero), first)
        return ((own_k, own_v, cross_k, cross_v), grad_q)
    empty = jnp.zeros((WINDOW + length, width), jnp.float32)
    (own_k, own_v, cross_k, cross_v), grad_qs = lax.scan(backward_block, (empty, empty, empty, empty), jnp.arange(count, dtype=jnp.int32))
    grad_keys = (own_k + lowered(cross_k))[WINDOW:].astype(jnp.bfloat16)
    grad_values = (own_v + lowered(cross_v))[WINDOW:].astype(jnp.bfloat16)
    grad_qkv = jnp.concatenate([grad_qs.reshape(length, width), grad_keys, grad_values], 1)
    grad_normed = jnp.dot(grad_qkv, w_qkv.T, preferred_element_type=jnp.float32)
    scaled = grad_normed * gain
    grad_x = grad_out.astype(jnp.float32) + (scaled - normal_x * lax.optimization_barrier(jnp.mean(scaled * normal_x, axis=1, keepdims=True))) * inv_rms
    term_qkv = lax.dot_general(normed, grad_qkv, (((0,), (0,)), ((), ())), preferred_element_type=jnp.float32)
    return (grad_x.astype(jnp.bfloat16), term_qkv)

def reference(inputs, cotangent, gain, w_qkv, w_out, segment_ids):
    grads = []
    total_qkv = jnp.zeros(w_qkv.shape, jnp.float32)
    for group in range(N_DP):
        grad_x, term_qkv = one_sequence(inputs[group], cotangent[group], gain, w_qkv, w_out, segment_ids[group])
        grads.append(grad_x)
        total_qkv = total_qkv + term_qkv
    return (jnp.stack(grads, 0), total_qkv / N_DP)
```

```python
import functools

import jax
import jax.numpy as jnp
from jax import lax
from jax.experimental import pallas as pl
from jax.experimental.pallas import tpu as pltpu
from jax.sharding import PartitionSpec as P

HEADS = 16
WINDOW = 512
EPS = 1e-05
TILE = 128
PACK = 2
GROUPS = (3, 3, 2)

F32, BF16 = jnp.float32, jnp.bfloat16
NT = (((1,), (1,)), ((), ()))
TN = (((0,), (0,)), ((), ()))


def shifted(array, axis, by):
    peers = lax.axis_size(axis)
    pairs = [(i, i + by) for i in range(peers) if 0 <= i + by < peers]
    return lax.ppermute(array, axis, pairs)


def swapped(array, axis, bit):
    peers = lax.axis_size(axis)
    return lax.ppermute(array, axis, [(i, i ^ (1 << bit)) for i in range(peers)])


def attention_kernel(
    rows, window, head, q_ref, k_ref, v_ref, kp_ref, vp_ref, do_ref, segq_ref, segk_ref,
    own_ref, cross_ref, bias, kext, vext, kt, dk, dv,
):
    scale = head ** -0.5
    span = window + TILE
    tiles = rows // TILE

    @pl.when(pl.program_id(0) == 0)
    def _():
        r = lax.broadcasted_iota(jnp.int32, (span, TILE), 0)
        c = lax.broadcasted_iota(jnp.int32, (span, TILE), 1)
        band = (r > c) & (r <= c + window)
        for t in range(tiles):
            seg_k = segk_ref[t * TILE : t * TILE + span, :]
            seg_q = segq_ref[:, t * TILE : (t + 1) * TILE]
            bias[t] = jnp.where(band & (seg_k == seg_q), 0.0, -1e30)

    kext[:window] = kp_ref[...]
    kext[window:] = k_ref[...]
    vext[:window] = vp_ref[...]
    vext[window:] = v_ref[...]
    kt[...] = kext[...].T
    dk[...] = jnp.zeros_like(dk)
    dv[...] = jnp.zeros_like(dv)
    lane = lax.broadcasted_iota(jnp.int32, (TILE, PACK * head), 1) // head
    row = lax.broadcasted_iota(jnp.int32, (PACK * head, TILE), 0) // head

    def spread(x):
        return jnp.concatenate([jnp.where(lane == h, x, jnp.zeros_like(x)) for h in range(PACK)], 0)

    for t in range(tiles):
        at, ext = pl.ds(t * TILE, TILE), pl.ds(t * TILE, span)
        qs = spread(q_ref[at, :] * jnp.asarray(scale, BF16))
        do = spread(do_ref[at, :])
        scores = lax.dot_general(kext[ext, :], qs, NT, preferred_element_type=F32)
        scores = scores + jnp.concatenate([bias[t]] * PACK, 1)
        expo = jnp.exp(scores - jnp.max(scores, axis=0, keepdims=True))
        probs = expo * (1.0 / jnp.sum(expo, axis=0, keepdims=True))
        dprob = lax.dot_general(vext[ext, :], do, NT, preferred_element_type=F32)
        delta = jnp.sum(probs * dprob, axis=0, keepdims=True)
        dscore = (probs * (dprob - delta)).astype(BF16)
        dv[ext, :] += jnp.dot(probs.astype(BF16), do, preferred_element_type=F32)
        dk[ext, :] += jnp.dot(dscore, qs, preferred_element_type=F32)
        dq = jnp.dot(kt[:, ext], dscore, preferred_element_type=F32)
        mine = dq[:, :TILE]
        for h in range(1, PACK):
            mine = jnp.where(row == h, dq[:, h * TILE : (h + 1) * TILE], mine)
        own_ref[0, at, :] = (mine.T * scale).astype(BF16)
    cross_ref[0] = dk[:window].astype(BF16)
    cross_ref[1] = dv[:window].astype(BF16)
    own_ref[1] = dk[window:].astype(BF16)
    own_ref[2] = dv[window:].astype(BF16)


def attention(qkv, kv_before, d_attn, seg_q, seg_k, first, pairs):
    rows, width = d_attn.shape
    head = width // HEADS
    lanes = PACK * head
    per = width // lanes
    cols = pairs * lanes
    ext = WINDOW + rows
    spec = pl.BlockSpec
    tiles = rows // TILE
    work = tiles * (WINDOW + TILE) * PACK * TILE
    return pl.pallas_call(
        functools.partial(attention_kernel, rows, WINDOW, head),
        grid=(pairs,),
        in_specs=[
            spec((rows, lanes), lambda i: (0, first + i)),
            spec((rows, lanes), lambda i: (0, per + first + i)),
            spec((rows, lanes), lambda i: (0, 2 * per + first + i)),
            spec((WINDOW, lanes), lambda i: (0, first + i)),
            spec((WINDOW, lanes), lambda i: (0, per + first + i)),
            spec((rows, lanes), lambda i: (0, first + i)),
            spec((1, rows), lambda i: (0, 0)),
            spec((ext, 1), lambda i: (0, 0)),
        ],
        out_specs=[
            spec((3, rows, lanes), lambda i: (0, 0, i)),
            spec((2, WINDOW, lanes), lambda i: (0, 0, i)),
        ],
        out_shape=[
            jax.ShapeDtypeStruct((3, rows, cols), BF16),
            jax.ShapeDtypeStruct((2, WINDOW, cols), BF16),
        ],
        scratch_shapes=[
            pltpu.VMEM((tiles, WINDOW + TILE, TILE), F32),
            pltpu.VMEM((ext, lanes), BF16),
            pltpu.VMEM((ext, lanes), BF16),
            pltpu.VMEM((lanes, ext), BF16),
            pltpu.VMEM((ext, lanes), F32),
            pltpu.VMEM((ext, lanes), F32),
        ],
        compiler_params=pltpu.CompilerParams(vmem_limit_bytes=40 * 2**20),
        cost_estimate=pl.CostEstimate(
            flops=pairs * work * 2 * 5 * lanes * 2,
            bytes_accessed=pairs * rows * lanes * 2 * 12,
            transcendentals=pairs * work,
        ),
        name="attention_backward",
    )(qkv, qkv, qkv, kv_before, kv_before, d_attn, seg_q, seg_k)


def bits_of(count):
    return count.bit_length() - 1


def scattered_sum(keep, send, axis, order):
    terms = [keep]
    for step, bit in enumerate(order):
        got = swapped(send, axis, bit)
        terms.append(got)
        if step + 1 < len(order):
            half = got.shape[0] // 2
            total = sum(term[half:].astype(F32) for term in terms)
            send = total.astype(BF16)
            terms = [term[:half] for term in terms]
    return sum(term.astype(F32) for term in terms)


def full_sum(value, axis):
    for bit in range(bits_of(lax.axis_size(axis))):
        low = lax.optimization_barrier(value.astype(BF16))
        value = low.astype(F32) + swapped(low, axis, bit).astype(F32)
    return value


def block_offsets(order):
    offsets = [0]
    for bit in reversed(order):
        offsets = offsets + [o | (1 << bit) for o in offsets]
    return offsets


def normalized(x_rows, gain):
    xf = x_rows.astype(F32)
    inv_rms = lax.rsqrt(jnp.mean(xf * xf, axis=1, keepdims=True) + EPS)
    normal_x = xf * inv_rms
    return normal_x, inv_rms, (normal_x * gain).astype(BF16)


def body(inputs, cotangent, gain, w_qkv, w_out, segment_ids):
    x_rows = inputs[0]
    grad_out = cotangent[0]
    rows, width = x_rows.shape
    x_before = shifted(x_rows[rows - WINDOW :], "seq", 1)
    normal_x, inv_rms, normed = normalized(x_rows, gain)
    qkv = jnp.dot(normed, w_qkv, preferred_element_type=F32).astype(BF16)
    d_attn = lax.dot_general(grad_out, w_out, NT, preferred_element_type=F32).astype(BF16)
    normed_before = normalized(x_before, gain)[2]
    kv_before = jnp.dot(normed_before, w_qkv[:, width:], preferred_element_type=F32).astype(BF16)

    me = lax.axis_index("seq")
    offset = me * rows
    seg_padded = jnp.concatenate([jnp.full((WINDOW,), -1, jnp.int32), segment_ids[0]], 0)
    seg_ext = lax.dynamic_slice_in_dim(seg_padded, offset, WINDOW + rows, 0)
    seg_k = seg_ext[:, None]
    seg_q = seg_ext[None, WINDOW:]

    peers = lax.axis_size("seq")
    order = list(range(bits_of(peers)))
    piece = width // peers
    around = jnp.concatenate(
        [lax.dynamic_slice_in_dim(normed, (me ^ o) * piece, piece, 1) for o in block_offsets(order)], 1
    )
    lanes = PACK * (width // HEADS)
    firsts = [sum(GROUPS[:g]) for g in range(len(GROUPS))]
    grads, totals = [], []
    for first, pairs in zip(firsts, GROUPS):
        own, cross = attention(qkv, kv_before, d_attn, seg_q, seg_k, first, pairs)
        back = shifted(cross, "seq", -1)
        later = [(own[n].astype(F32)).at[rows - WINDOW :].add(back[n - 1].astype(F32)).astype(BF16) for n in (1, 2)]
        grad = jnp.concatenate([own[0]] + later, 1)
        grads.append(grad)
        half = width // 2
        send = lax.dot_general(around[:, half:], grad, TN, preferred_element_type=F32).astype(BF16)
        keep = lax.dot_general(around[:, :half], grad, TN, preferred_element_type=F32).astype(BF16)
        totals.append(full_sum(scattered_sum(keep, send, "seq", order), "dp"))
    parts = []
    for n in range(3):
        for grad, first, pairs in zip(grads, firsts, GROUPS):
            parts.append(grad[:, n * pairs * lanes : (n + 1) * pairs * lanes])
    grad_qkv = jnp.concatenate(parts, 1)
    grad_normed = lax.dot_general(grad_qkv, w_qkv, NT, preferred_element_type=F32)
    scaled = grad_normed * gain
    grad_x = (
        grad_out.astype(F32)
        + (scaled - normal_x * jnp.mean(scaled * normal_x, axis=1, keepdims=True)) * inv_rms
    )
    parts = []
    for n in range(3):
        for total, first, pairs in zip(totals, firsts, GROUPS):
            parts.append(total[:, n * pairs * lanes : (n + 1) * pairs * lanes])
    factor = 1.0 / lax.axis_size("dp")
    return (grad_x.astype(BF16)[None], jnp.concatenate(parts, 1) * factor)


def solution(mesh):
    return jax.shard_map(
        body,
        mesh=mesh,
        in_specs=(P("dp", "seq", None), P("dp", "seq", None), P(), P(), P(), P("dp", None)),
        out_specs=(P("dp", "seq", None), P("seq", None)),
        check_vma=False,
    )
```
